512 devices in a mesh: dp: 32 (over x, z_lo, core), frame: 16 (over z_hi, y).
Axes of the slice: x: 4, y: 4, z: 16 (z_hi: 4, z_lo: 4; z = z_hi * 4 + z_lo), core: 2. Of those that a mesh axis runs over, the one named last changes fastest.
Arguments:
- queries: bfloat16 [32, 16, 128, 2048], P('dp', 'frame'), may hold values from -12 to 12
- key_states: bfloat16 [32, 16, 128, 2048], P('dp', 'frame'), may hold values from -6 to 6
- value_states: bfloat16 [32, 16, 128, 2048], P('dp', 'frame'), may hold values from -6 to 6
- head_scale: float32 [16], replicated, may hold values from 0.5 to 4
- out_weight: bfloat16 [2048, 3072], P('dp'), may hold values from -0.125 to 0.125
- frame_pattern: int32 [16, 2], replicated, may hold values from 0 to 15, as said below
- out_grad: bfloat16 [32, 16, 128, 3072], P('dp', 'frame'), may hold values from -6 to 6
Outputs:
- attended: bfloat16 [32, 16, 128, 3072], P('dp', 'frame')
- query_grad: bfloat16 [32, 16, 128, 2048], P('dp', 'frame')
- key_grad: bfloat16 [32, 16, 128, 2048], P('dp', 'frame')
- value_grad: bfloat16 [32, 16, 128, 2048], P('dp', 'frame')
- scale_grad: float32 [16], replicated
The draws below stay inside these ranges and needn't reach their ends.
Inputs may be any that keep to these rules, and one draw needn't show every extreme that they name: `frame_pattern`: row f names 2 different frames, the first of them f itself.
All inputs are finite; a program needn't handle non-finite values.
Results may differ from the reference program's by a relative error of at most 0.0058.
Values may be sent and summed in bfloat16 or wider, within the bound.
A program may use at most 128 MiB of HBM per device.

```python
import math
import jax
import jax.numpy as jnp
from jax import lax

D = 3072
H = 16
HDH = 128
TOK = 128
HD = 2048
FRAMES = 16
SLOTS = 2
CLIPS = 32


def key_field(key):
    shape = (CLIPS, FRAMES, TOK, H * HDH)
    field = jnp.clip(jax.random.normal(jax.random.fold_in(key, 11), shape, jnp.float32), -6.0, 6.0)
    return field


def draw_key_states(key, part):
    return key_field(key).astype(jnp.bfloat16)


def draw_queries(key, part):
    shape = (CLIPS, FRAMES, TOK, H * HDH)
    base = jnp.clip(jax.random.normal(jax.random.fold_in(key, 12), shape, jnp.float32), -6.0, 6.0)
    return base.astype(jnp.bfloat16)


def draw_frame_pattern(key, part):
    frames = jnp.arange(FRAMES, dtype=jnp.int32)
    subkeys = jax.random.split(jax.random.fold_in(key, 21), FRAMES)
    orders = jax.vmap(lambda single: jax.random.permutation(single, FRAMES - 1))(subkeys).astype(jnp.int32)
    others = orders + (orders >= frames[:, None]).astype(jnp.int32)
    return jnp.concatenate([frames[:, None], others[:, :SLOTS - 1]], axis=1).astype(jnp.int32)


def levels(rng, dims, cuts, low, largest):
    def one(dim, shards_of):
        steps = jax.random.uniform(jax.random.fold_in(jax.random.fold_in(rng, 6), dim), (shards_of,), jnp.float32, low / len(cuts), largest / len(cuts))
        return jnp.repeat(jnp.exp(steps), dims[dim] // shards_of).reshape((-1,) + (1,) * (len(dims) - dim - 1))

    factor_of = one(*cuts[0])
    for cut in cuts[1:]:
        factor_of = factor_of * one(*cut)
    return factor_of


def centred(own_key, shape, scale, most, pieces=(), kind=jnp.bfloat16):
    result = scale * jax.random.normal(own_key, shape, jnp.float32)
    if pieces:
        result = result * levels(own_key, shape, pieces, -0.22, 0.18)
    return jnp.clip(result, -most, most).astype(kind)


def setup_inputs(seed: int = 0) -> dict:
    arg_keys = jax.random.split(jax.random.key(seed), 8)
    return {
        "queries": draw_queries(jax.random.fold_in(arg_keys[7], 71), 0),
        "key_states": draw_key_states(jax.random.fold_in(arg_keys[7], 71), 0),
        "value_states": centred(arg_keys[2], (CLIPS, FRAMES, TOK, HD), 1.0, 6.0, ((0, 32), (1, 16))),
        "head_scale": jnp.clip(jnp.exp(jax.random.uniform(arg_keys[3], (H,), jnp.float32, math.log(0.5), math.log(4.0))), 0.5, 4.0),
        "out_weight": centred(arg_keys[4], (HD, D), HD ** -0.5, 0.125, ((0, 32),)),
        "frame_pattern": draw_frame_pattern(jax.random.fold_in(arg_keys[7], 71), 0),
        "out_grad": centred(arg_keys[6], (CLIPS, FRAMES, TOK, D), 1.0, 6.0, ((0, 32), (1, 16))),
    }


def head_pass(queries, key_states, value_states, out_grad, head_scale, out_weight, frame_pattern):
    frames = queries.shape[0]
    tokens = queries.shape[1]
    inv_root = 1.0 / math.sqrt(HDH)
    factor = head_scale * inv_root
    query_heads = queries.reshape(frames, tokens, H, HDH).astype(jnp.float32)
    key_sel = key_states[frame_pattern].reshape(frames, SLOTS * tokens, H, HDH).astype(jnp.float32)
    value_sel = value_states[frame_pattern].reshape(frames, SLOTS * tokens, H, HDH).astype(jnp.float32)
    plain_scores = jnp.einsum('fthd,fkhd->fhtk', query_heads, key_sel, precision=lax.Precision.HIGHEST)
    probs = jax.nn.softmax(plain_scores * factor[None, :, None, None], axis=-1)
    probs_low = lax.optimization_barrier(probs.astype(jnp.bfloat16)).astype(jnp.float32)
    context = jnp.einsum('fhtk,fkhd->fthd', probs_low, value_sel, precision=lax.Precision.HIGHEST).astype(jnp.bfloat16)
    context_rows = context.reshape(frames * tokens, H * HDH)
    attended = jnp.dot(context_rows, out_weight, preferred_element_type=jnp.float32).astype(jnp.bfloat16)
    grad_rows = out_grad.reshape(frames * tokens, out_grad.shape[2])
    context_grad = lax.dot_general(grad_rows, out_weight, (((1,), (1,)), ((), ())), preferred_element_type=jnp.float32).astype(jnp.bfloat16)
    grad_heads = context_grad.reshape(frames, tokens, H, HDH).astype(jnp.float32)
    prob_grad = jnp.einsum('fthd,fkhd->fhtk', grad_heads, value_sel, precision=lax.Precision.HIGHEST)
    score_grad = probs * (prob_grad - lax.optimization_barrier(jnp.sum(prob_grad * probs, axis=-1, keepdims=True)))
    scale_part = lax.optimization_barrier(jnp.sum(score_grad * plain_scores, axis=(0, 2, 3))) * inv_root
    score_low = lax.optimization_barrier(score_grad.astype(jnp.bfloat16)).astype(jnp.float32)
    query_grad = jnp.einsum('fhtk,fkhd->fthd', score_low, key_sel, precision=lax.Precision.HIGHEST) * factor[None, None, :, None]
    query_grad = query_grad.astype(jnp.bfloat16).reshape(frames, tokens, H * HDH)
    key_part = jnp.einsum('fhtk,fthd->fkhd', score_low, query_heads, precision=lax.Precision.HIGHEST) * factor[None, None, :, None]
    key_part = key_part.reshape(frames, SLOTS, tokens, H * HDH)
    key_grad = jnp.zeros((frames, tokens, H * HDH), jnp.float32).at[frame_pattern].add(key_part).astype(jnp.bfloat16)
    value_part = jnp.einsum('fhtk,fthd->fkhd', probs_low, grad_heads, precision=lax.Precision.HIGHEST)
    value_part = value_part.reshape(frames, SLOTS, tokens, H * HDH)
    value_grad = jnp.zeros((frames, tokens, H * HDH), jnp.float32).at[frame_pattern].add(value_part).astype(jnp.bfloat16)
    return (attended.reshape(frames, tokens, out_weight.shape[1]), query_grad, key_grad, value_grad, scale_part)

def reference(queries, key_states, value_states, head_scale, out_weight, frame_pattern, out_grad):

    def one_clip(items):
        return head_pass(items[0], items[1], items[2], items[3], head_scale, out_weight, frame_pattern)
    results = lax.map(one_clip, (queries, key_states, value_states, out_grad))
    scale_grad = lax.optimization_barrier(jnp.sum(results[4], axis=0))
    return (results[0], results[1], results[2], results[3], scale_grad)
```

```python
import math

import jax
import jax.numpy as jnp
from jax import lax
from jax.experimental import pallas as pl
from jax.experimental.pallas import tpu as pltpu
from jax.sharding import PartitionSpec as P

MESH = pl.DeviceIdType.MESH
F = 16
T = 128
HDH = 128
D = 3072
HALF = D // 2
BF16 = jnp.bfloat16
F32 = jnp.float32

A, B1Y, B1X, Q, K, V, CG, CX, QG, KG, VG = range(11)
B2X, B2Y, SIB, RED = 11, 14, 17, 25
N_SEM = 30
NT = (((1,), (1,)), ((), ()))
TN = (((0,), (0,)), ((), ()))


def body(
    pat, scale, q, k, v, og, w, att, qg, kg, vg, sg,
    wv, ogv, qb, kb, vb, cb, cgo, cxo, cxr, qo, ko, vo, kp, vp, plain, probs, attv, red, redo,
    ss, rs, ls,
):
    d, f = lax.axis_index("dp"), lax.axis_index("frame")
    x, zl, core = d // 8, lax.rem(d // 2, 4), lax.rem(d, 2)
    zh, y = f // 4, lax.rem(f, 4)
    z = zh * 4 + zl

    def at_frame(i):
        return (d, lax.rem(f + i, F))

    def at_x(i):
        return (lax.rem(x + i + 4, 4) * 8 + lax.rem(d, 8), f)

    def at_y(i):
        return (d, zh * 4 + lax.rem(y + i + 4, 4))

    def at_zh(i):
        return (d, lax.rem(zh + i + 4, 4) * 4 + y)

    def at_z(i):
        there = lax.rem(z + i + 16, 16)
        return (x * 8 + lax.rem(there, 4) * 2 + core, (there // 4) * 4 + y)

    sibling = (d + 1 - 2 * core, f)

    def send(src, dst, sem, device, recv=None):
        pltpu.make_async_remote_copy(
            src, dst, ss.at[sem], rs.at[sem if recv is None else recv], device_id=device, device_id_type=MESH
        ).start()

    def arrive(sem, ref):
        pltpu.make_async_copy(ref, ref, rs.at[sem]).wait()

    def sent(sem, ref):
        pltpu.make_async_copy(ref, ref, ss.at[sem]).wait()

    barrier = pltpu.get_barrier_semaphore()
    peers = [at_x(i) for i in (1, 2, 3)] + [at_z(i) for i in (1, -1, 2, -2)] + [sibling]

    @pl.loop(1, F)
    def _(i):
        pl.semaphore_signal(barrier, inc=1, device_id=at_frame(i), device_id_type=MESH)

    for peer in peers:
        pl.semaphore_signal(barrier, inc=1, device_id=peer, device_id_type=MESH)
    pl.semaphore_wait(barrier, F - 1 + len(peers))

    rows = pl.ds(pl.multiple_of(y * 16, 16), 16)
    first, second = pl.ds(0, HALF), pl.ds(HALF, HALF)
    mine = pl.ds(pl.multiple_of(f * HDH, HDH), HDH)

    for i in (1, -1, 2):
        send(w.at[rows], wv.at[x, zl, core, rows], A, at_z(i))
    pltpu.make_async_copy(w.at[rows], wv.at[x, zl, core, rows], rs.at[A]).start()
    pltpu.make_async_copy(og, ogv, ls.at[0]).start()

    def scatter(src, dst, sem):
        @pl.loop(1, F)
        def _(i):
            there = lax.rem(f + i, F)
            send(src.at[:, pl.ds(pl.multiple_of(there * HDH, HDH), HDH)], dst.at[f], sem, (d, there))

        pltpu.make_async_copy(src.at[:, mine], dst.at[f], rs.at[sem]).start()

    scatter(q, qb, Q)

    arrive(A, wv.at[x, :, core, rows])
    for i in (1, 2, 3):
        send(wv.at[x, :, core, rows, first], wv.at[x, :, core, rows, first], B1Y, at_y(i))
        send(wv.at[x, :, core, rows, second], wv.at[x, :, core, rows, second], B1X, at_x(i))
    scatter(k, kb, K)

    arrive(B1Y, wv.at[x, :, core, pl.ds(0, 48), first])
    for i in (1, 2, 3):
        send(wv.at[x, :, core, :, first], wv.at[x, :, core, :, first], B2X + i - 1, at_x(i))
    send(wv.at[x, :, core, :, first], wv.at[x, :, core, :, first], SIB, sibling)
    arrive(B1X, wv.at[pl.ds(0, 3), :, core, rows, second])
    for i in (1, 2, 3):
        send(wv.at[:, :, core, rows, second], wv.at[:, :, core, rows, second], B2Y + i - 1, at_y(i))
    send(wv.at[:, :, core, rows, second], wv.at[:, :, core, rows, second], SIB + 1, sibling)
    scatter(v, vb, V)

    for i in (1, 2, 3):
        there = lax.rem(x - i + 4, 4)
        piece = wv.at[there, :, core, :, first]
        arrive(B2X + i - 1, piece)
        send(piece, piece, SIB + 1 + i, sibling)
        there = pl.ds(pl.multiple_of(lax.rem(y - i + 4, 4) * 16, 16), 16)
        piece = wv.at[:, :, core, there, second]
        arrive(B2Y + i - 1, piece)
        send(piece, piece, SIB + 4 + i, sibling)
    for i in range(8):
        arrive(SIB + i, wv.at[0, :, core, :, first])
    pltpu.make_async_copy(og, ogv, ls.at[0]).wait()

    def context_grad(pair):
        two = wv[pair // 2, pl.ds(lax.rem(pair, 2) * 2, 2)].reshape(2 * HDH, D)
        made = lax.dot_general(ogv[...], two, NT, preferred_element_type=F32).astype(BF16)
        return made[:, :HDH], made[:, HDH:]

    @pl.loop(1, F // 2)
    def _(i):
        pair = lax.rem(f // 2 + i, F // 2)
        even, odd = context_grad(pair)
        cgo[2 * pair] = even
        send(cgo.at[2 * pair], cb.at[f], CG, (d, 2 * pair))
        cgo[2 * pair + 1] = odd
        send(cgo.at[2 * pair + 1], cb.at[f], CG, (d, 2 * pair + 1))

    own, other = f, f + 1 - 2 * lax.rem(f, 2)
    even, odd = context_grad(f // 2)
    cgo[2 * (f // 2)] = even
    cgo[2 * (f // 2) + 1] = odd
    send(cgo.at[other], cb.at[f], CG, (d, other))
    cb[f] = cgo[own]

    inv_root = 1.0 / math.sqrt(HDH)
    factor = scale[f] * inv_root
    for sem, ref in ((Q, qb), (K, kb), (V, vb)):
        arrive(sem, ref)

    def both(ref, t):
        return jnp.concatenate([ref[t], ref[pat[t, 1]]], axis=0)

    def forward(t):
        scores = lax.dot_general(both(kb, t), qb[t], NT, preferred_element_type=F32)
        plain[t] = scores
        scaled = scores * factor
        e = jnp.exp(scaled - jnp.max(scaled, axis=0, keepdims=True))
        p = e / jnp.sum(e, axis=0, keepdims=True)
        probs[t] = p
        return lax.dot_general(p.astype(BF16), both(vb, t), TN, preferred_element_type=F32).astype(BF16)

    @pl.loop(1, F)
    def _(i):
        t = lax.rem(f + i, F)
        cxo[t] = forward(t)
        send(cxo.at[t], cxr.at[:, mine], CX, (d, t))

    cxr[:, mine] = forward(f)

    arrive(CG, cb.at[pl.ds(0, F - 1)])

    def backward(t):
        p = probs[t]
        gain = cb[t]
        prob_grad = lax.dot_general(both(vb, t), gain, NT, preferred_element_type=F32)
        score_grad = p * (prob_grad - jnp.sum(prob_grad * p, axis=0, keepdims=True))
        term = jnp.sum((score_grad * plain[t]).reshape(32, 8, HDH), axis=0)
        low = score_grad.astype(BF16)
        query = lax.dot_general(low, both(kb, t), TN, preferred_element_type=F32) * factor
        key = jnp.dot(low, qb[t], preferred_element_type=F32) * factor
        value = jnp.dot(p.astype(BF16), gain, preferred_element_type=F32)
        kp[0, t], kp[1, t] = key[:T], key[T:]
        vp[0, t], vp[1, t] = value[:T], value[T:]
        qo[t] = query.astype(BF16)
        return term

    redo[0] = jnp.zeros((8, HDH), F32)

    @pl.loop(1, F)
    def _(i):
        t = lax.rem(f + i, F)
        redo[0] += backward(t)
        send(qo.at[t], qg.at[:, mine], QG, (d, t))

    total = jnp.sum(redo[0] + backward(f), keepdims=True) * inv_root
    pltpu.make_async_copy(qo.at[f], qg.at[:, mine], ls.at[1]).start()

    lanes = lax.broadcasted_iota(jnp.int32, (8, HDH), 1)
    stages = (
        (2, core, [sibling]),
        (4, x, [at_x(i) for i in (1, 2, 3)]),
        (4, y, [at_y(i) for i in (1, 2, 3)]),
        (4, zh, [at_zh(i) for i in (1, 2, 3)]),
        (4, zl, [at_z(i) for i in (1, -1, 2)]),
    )

    def give(s, value):
        _, here, devices = stages[s]
        redo[s + 1] = value
        red[s, here] = value
        for device in devices:
            send(redo.at[s + 1], red.at[s, here], RED + s, device)

    def take(s):
        n, _, devices = stages[s]
        arrive(RED + s, red.at[s, pl.ds(0, len(devices))])
        return sum(red[s, j] for j in range(1, n)) + red[s, 0]

    give(0, jnp.where(lanes == f, total, 0.0))

    def gather(part, out, dst, sem, local):
        def one(g):
            acc = part[0, g]
            for t in range(F):
                acc += jnp.where(pat[t, 1] == g, 1.0, 0.0) * part[1, t]
            out[g] = acc.astype(BF16)

        @pl.loop(1, F)
        def _(i):
            g = lax.rem(f + i, F)
            one(g)
            send(out.at[g], dst.at[:, mine], sem, (d, g))

        one(f)
        pltpu.make_async_copy(out.at[f], dst.at[:, mine], ls.at[local]).start()

    gather(kp, ko, kg, KG, 2)
    give(1, take(0))
    gather(vp, vo, vg, VG, 3)
    give(2, take(1))

    arrive(CX, cxr.at[:, pl.ds(0, (F - 1) * HDH)])
    width = 512

    @pl.loop(0, D // width)
    def _(n):
        cols = pl.ds(pl.multiple_of(n * width, width), width)
        block = wv[:, :, :, :, cols].reshape(F * HDH, width)
        attv[:, cols] = jnp.dot(cxr[...], block, preferred_element_type=F32).astype(BF16)

    pltpu.make_async_copy(attv, att, ls.at[4]).start()
    give(3, take(2))
    give(4, take(3))
    sg[...] = take(4)[:1, :F]

    for sem, ref in ((QG, qg), (KG, kg), (VG, vg)):
        arrive(sem, ref.at[:, pl.ds(0, (F - 1) * HDH)])
    for j, (src, dst) in enumerate(((qo, qg), (ko, kg), (vo, vg))):
        pltpu.make_async_copy(src.at[f], dst.at[:, mine], ls.at[j + 1]).wait()
    pltpu.make_async_copy(attv, att, ls.at[4]).wait()
    for sem, ref in ((Q, qb), (K, kb), (V, vb), (CG, cgo), (CX, cxo), (QG, qo), (KG, ko), (VG, vo)):
        sent(sem, ref.at[pl.ds(0, F - 1)])
    sent(A, wv.at[0, pl.ds(0, 3), 0, pl.ds(0, 16)])
    sent(B1Y, wv.at[0, :, 0, pl.ds(0, 48), first])
    sent(B1X, wv.at[pl.ds(0, 3), :, 0, pl.ds(0, 16), second])
    for i in range(3):
        sent(B2X + i, wv.at[0, :, 0, :, first])
        sent(B2Y + i, wv.at[:, :, 0, pl.ds(0, 16), second])
    for i in range(8):
        sent(SIB + i, wv.at[0, :, 0, :, first])
    for s, (_, _, devices) in enumerate(stages):
        sent(RED + s, red.at[s, pl.ds(0, len(devices))])


def local(queries, key_states, value_states, head_scale, out_weight, frame_pattern, out_grad):
    anywhere = pl.BlockSpec(memory_space=pl.ANY)
    scalars = pl.BlockSpec(memory_space=pltpu.SMEM)
    slots = pltpu.VMEM((F, T, HDH), BF16)
    parts = pltpu.VMEM((2, F, T, HDH), F32)
    square = pltpu.VMEM((F, 2 * T, T), F32)
    row = jax.ShapeDtypeStruct((T, F * HDH), BF16)
    attended, query_grad, key_grad, value_grad, scale_grad = pl.pallas_call(
        body,
        out_shape=(
            jax.ShapeDtypeStruct((T, D), BF16),
            row,
            row,
            row,
            jax.ShapeDtypeStruct((1, F), F32),
        ),
        in_specs=[scalars, scalars] + [anywhere] * 5,
        out_specs=[anywhere] * 4 + [pl.BlockSpec(memory_space=pltpu.VMEM)],
        scratch_shapes=[
            pltpu.VMEM((4, 4, 2, 64, D), BF16),
            pltpu.VMEM((T, D), BF16),
            slots, slots, slots, slots,
            slots, slots,
            pltpu.VMEM((T, F * HDH), BF16),
            slots, slots, slots,
            parts, parts,
            square, square,
            pltpu.VMEM((T, D), BF16),
            pltpu.VMEM((5, 4, 8, HDH), F32),
            pltpu.VMEM((6, 8, HDH), F32),
            pltpu.SemaphoreType.DMA((N_SEM,)),
            pltpu.SemaphoreType.DMA((N_SEM,)),
            pltpu.SemaphoreType.DMA((5,)),
        ],
        compiler_params=pltpu.CompilerParams(
            collective_id=0, has_side_effects=True, vmem_limit_bytes=56 << 20
        ),
    )(
        frame_pattern,
        head_scale,
        queries[0, 0],
        key_states[0, 0],
        value_states[0, 0],
        out_grad[0, 0],
        out_weight,
    )
    return (
        attended[None, None],
        query_grad[None, None],
        key_grad[None, None],
        value_grad[None, None],
        scale_grad.reshape(F),
    )


def solution(mesh):
    rows = P("dp", "frame", None, None)
    return jax.shard_map(
        local,
        mesh=mesh,
        in_specs=(rows, rows, rows, P(), P("dp", None), P(), rows),
        out_specs=(rows, rows, rows, rows, P()),
        check_vma=False,
    )
```

```python
import math

import jax
import jax.numpy as jnp
from jax import lax
from jax.experimental import pallas as pl
from jax.experimental.pallas import tpu as pltpu
from jax.sharding import PartitionSpec as P

MESH = pl.DeviceIdType.MESH
F = 16
T = 128
HDH = 128
D = 3072
HALF = D // 2
BF16 = jnp.bfloat16
F32 = jnp.float32

A, B1Y, B1X, OG, Q, K, V, CG, CX, ATT, QG, KG, VG = range(13)
B2X, B2Y, RED = 13, 16, 19
N_SEM = 24
NT = (((1,), (1,)), ((), ()))
TN = (((0,), (0,)), ((), ()))


def body(
    pat, scale, q, k, v, og, w, att, qg, kg, vg, sg,
    wv, ogv, qb, kb, vb, cb, cgo, cxo, cxr, qo, ko, vo, kp, vp, plain, probs, attp, attr, attv, red, redo,
    ss, rs, ls,
):
    d, f = lax.axis_index("dp"), lax.axis_index("frame")
    x, zl, core = d // 8, lax.rem(d // 2, 4), lax.rem(d, 2)
    zh, y = f // 4, lax.rem(f, 4)
    z = zh * 4 + zl

    def at_frame(i):
        return (d, lax.rem(f + i, F))

    def at_x(i):
        return (lax.rem(x + i + 4, 4) * 8 + lax.rem(d, 8), f)

    def at_y(i):
        return (d, zh * 4 + lax.rem(y + i + 4, 4))

    def at_zh(i):
        return (d, lax.rem(zh + i + 4, 4) * 4 + y)

    def at_z(i, c=core):
        there = lax.rem(z + i + 16, 16)
        return (x * 8 + lax.rem(there, 4) * 2 + c, (there // 4) * 4 + y)

    sibling = (d + 1 - 2 * core, f)

    def on_core(c, t):
        return (d - core + c, t)

    def turn(i):
        m = lax.rem(i, 4)
        dz = 1 + 2 * m - 3 * (m // 2)
        return lax.rem(zh + dz, 4) * 4 + lax.rem(y + 1 + i // 4, 4)

    def send(src, dst, sem, device, recv=None):
        pltpu.make_async_remote_copy(
            src, dst, ss.at[sem], rs.at[sem if recv is None else recv], device_id=device, device_id_type=MESH
        ).start()

    def arrive(sem, ref):
        pltpu.make_async_copy(ref, ref, rs.at[sem]).wait()

    def sent(sem, ref):
        pltpu.make_async_copy(ref, ref, ss.at[sem]).wait()

    barrier = pltpu.get_barrier_semaphore()
    peers = [at_x(i) for i in (1, 2, 3)] + [at_z(i, c) for i in (1, -1, 2, -2) for c in (0, 1)] + [sibling]

    @pl.loop(1, F)
    def _(i):
        t = lax.rem(f + i, F)
        for c in (0, 1):
            pl.semaphore_signal(barrier, inc=1, device_id=on_core(c, t), device_id_type=MESH)

    for peer in peers:
        pl.semaphore_signal(barrier, inc=1, device_id=peer, device_id_type=MESH)
    pl.semaphore_wait(barrier, 2 * (F - 1) + len(peers))

    rows = pl.ds(pl.multiple_of(y * 16, 16), 16)
    first, second = pl.ds(0, HALF), pl.ds(HALF, HALF)
    mine = pl.ds(pl.multiple_of(f * HDH, HDH), HDH)

    keeper = zl // 2
    quarter = wv.at[x, lax.rem(zl, 2), core, rows]
    for i in (1, -1, 2):
        send(w.at[rows], quarter, A, at_z(i, keeper))

    @pl.when(core == keeper)
    def _():
        pltpu.make_async_copy(w.at[rows], quarter, rs.at[A]).start()

    @pl.when(core != keeper)
    def _():
        send(w.at[rows], quarter, A, sibling)

    pltpu.make_async_copy(og, ogv.at[core], ls.at[0]).start()
    send(og, ogv.at[core], OG, sibling)

    def scatter(src, dst, sem):
        @pl.loop(0, F - 1)
        def _(i):
            there = turn(i)
            send(src.at[:, pl.ds(pl.multiple_of(there * HDH, HDH), HDH)], dst.at[f], sem, (d, there))

        pltpu.make_async_copy(src.at[:, mine], dst.at[f], rs.at[sem]).start()

    scatter(q, qb, Q)

    arrive(A, wv.at[x, :, :, rows])
    for i in (1, 2, 3):
        send(wv.at[x, :, :, rows, first], wv.at[x, :, :, rows, first], B1Y, at_y(i))
        send(wv.at[x, :, :, rows, second], wv.at[x, :, :, rows, second], B1X, at_x(i))
    scatter(k, kb, K)

    arrive(B1Y, wv.at[x, :, :, pl.ds(0, 48), first])
    for i in (1, 2, 3):
        send(wv.at[x, :, :, :, first], wv.at[x, :, :, :, first], B2X + i - 1, at_x(i))
    arrive(B1X, wv.at[pl.ds(0, 3), :, :, rows, second])
    for i in (1, 2, 3):
        send(wv.at[:, :, :, rows, second], wv.at[:, :, :, rows, second], B2Y + i - 1, at_y(i))
    scatter(v, vb, V)

    inv_root = 1.0 / math.sqrt(HDH)
    factor = scale[f] * inv_root

    here = pl.ds(pl.multiple_of((zh * 2 + lax.rem(y, 2)) * HDH, HDH), HDH)

    def both(ref, t):
        return jnp.concatenate([ref[t], ref[pat[1, t]]], axis=0)

    arrive(Q, qb)
    arrive(K, kb)

    @pl.loop(0, F)
    def _(t):
        scores = lax.dot_general(both(kb, t), qb[t], NT, preferred_element_type=F32)
        plain[t] = scores
        scaled = scores * factor
        e = jnp.exp(scaled - jnp.max(scaled, axis=0, keepdims=True))
        probs[t] = e / jnp.sum(e, axis=0, keepdims=True)

    arrive(V, vb)

    def forward(t):
        return lax.dot_general(probs[t].astype(BF16), both(vb, t), TN, preferred_element_type=F32).astype(BF16)

    @pl.loop(0, F - 1)
    def _(i):
        t = turn(i)
        cxo[t] = forward(t)
        send(cxo.at[t], cxr.at[core, :, here], CX, on_core(y // 2, t))

    cxo[f] = forward(f)

    @pl.when(core == y // 2)
    def _():
        pltpu.make_async_copy(cxo.at[f], cxr.at[core, :, here], rs.at[CX]).start()

    @pl.when(core != y // 2)
    def _():
        send(cxo.at[f], cxr.at[core, :, here], CX, sibling)

    for i in (1, 2, 3):
        arrive(B2X + i - 1, wv.at[0, :, :, :, first])
        arrive(B2Y + i - 1, wv.at[:, :, :, pl.ds(0, 16), second])
    pltpu.make_async_copy(og, ogv.at[core], ls.at[0]).wait()
    arrive(OG, ogv.at[0])

    @pl.loop(0, 4)
    def _(i):
        dz = 1 + 2 * i - 3 * (i // 2)
        zh_head = lax.rem(zh + dz, 4)
        two = wv[zh_head].reshape(2 * HDH, D)
        made = lax.dot_general(ogv[...].reshape(2 * T, D), two, NT, preferred_element_type=F32).astype(BF16)
        for e in (0, 1):
            head = zh_head * 4 + 2 * core + e
            for c in (0, 1):
                piece = cgo.at[c, 2 * zh_head + e]
                piece[...] = made[c * T : (c + 1) * T, e * HDH : (e + 1) * HDH]
                stays = jnp.logical_and(core == c, head == f)

                @pl.when(stays)
                def _():
                    pltpu.make_async_copy(piece, cb.at[f], rs.at[CG]).start()

                @pl.when(jnp.logical_not(stays))
                def _():
                    send(piece, cb.at[f], CG, on_core(c, head))

    arrive(CG, cb)

    def backward(t):
        p = probs[t]
        gain = cb[t]
        prob_grad = lax.dot_general(both(vb, t), gain, NT, preferred_element_type=F32)
        score_grad = p * (prob_grad - jnp.sum(prob_grad * p, axis=0, keepdims=True))
        term = jnp.sum((score_grad * plain[t]).reshape(32, 8, HDH), axis=0)
        low = score_grad.astype(BF16)
        query = lax.dot_general(low, both(kb, t), TN, preferred_element_type=F32) * factor
        key = jnp.dot(low, qb[t], preferred_element_type=F32) * factor
        value = jnp.dot(p.astype(BF16), gain, preferred_element_type=F32)
        kp[0, t], kp[1, t] = key[:T], key[T:]
        vp[0, t], vp[1, t] = value[:T], value[T:]
        qo[t] = query.astype(BF16)
        return term

    redo[0] = jnp.zeros((8, HDH), F32)

    @pl.loop(0, F - 1)
    def _(i):
        t = turn(i)
        redo[0] += backward(t)
        send(qo.at[t], qg.at[:, mine], QG, (d, t))

    total = jnp.sum(redo[0] + backward(f), keepdims=True) * inv_root
    pltpu.make_async_copy(qo.at[f], qg.at[:, mine], ls.at[1]).start()

    lanes = lax.broadcasted_iota(jnp.int32, (8, HDH), 1)
    stages = (
        (2, core, [sibling]),
        (4, x, [at_x(i) for i in (1, 2, 3)]),
        (4, y, [at_y(i) for i in (1, 2, 3)]),
        (4, zh, [at_zh(i) for i in (1, 2, 3)]),
        (4, zl, [at_z(i) for i in (1, -1, 2)]),
    )

    def give(s, value):
        _, here, devices = stages[s]
        redo[s + 1] = value
        red[s, here] = value
        for device in devices:
            send(redo.at[s + 1], red.at[s, here], RED + s, device)

    def take(s):
        n, _, devices = stages[s]
        arrive(RED + s, red.at[s, pl.ds(0, len(devices))])
        return sum(red[s, j] for j in range(1, n)) + red[s, 0]

    give(0, jnp.where(lanes == f, total, 0.0))

    def gather(part, out, dst, sem, local):
        def one(g):
            acc = part[0, g]
            for t in range(F):
                acc += jnp.where(pat[1, t] == g, 1.0, 0.0) * part[1, t]
            out[g] = acc.astype(BF16)

        @pl.loop(0, F - 1)
        def _(i):
            g = turn(i)
            one(g)
            send(out.at[g], dst.at[:, mine], sem, (d, g))

        one(f)
        pltpu.make_async_copy(out.at[f], dst.at[:, mine], ls.at[local]).start()

    gather(kp, ko, kg, KG, 2)
    give(1, take(0))
    gather(vp, vo, vg, VG, 3)
    give(2, take(1))

    arrive(CX, cxr)
    width = 512

    @pl.loop(0, D // width)
    def _(n):
        cols = pl.ds(pl.multiple_of(n * width, width), width)
        block = wv[:, :, :, :, cols].reshape(F // 2 * HDH, width)
        made = jnp.dot(cxr[...].reshape(2 * T, F // 2 * HDH), block, preferred_element_type=F32)
        attp[:, :, cols] = made.reshape(2, T, width)

    send(attp.at[1 - core], attr, ATT, sibling)

    arrive(ATT, attr)
    attv[...] = (attp[core] + attr[...]).astype(BF16)
    pltpu.make_async_copy(attv, att, ls.at[4]).start()
    give(3, take(2))
    give(4, take(3))
    sg[...] = take(4)[:1, :F]

    for sem, ref in ((QG, qg), (KG, kg), (VG, vg)):
        arrive(sem, ref.at[:, pl.ds(0, (F - 1) * HDH)])
    for j, (src, dst) in enumerate(((qo, qg), (ko, kg), (vo, vg))):
        pltpu.make_async_copy(src.at[f], dst.at[:, mine], ls.at[j + 1]).wait()
    pltpu.make_async_copy(attv, att, ls.at[4]).wait()
    for sem, ref in ((Q, qb), (K, kb), (V, vb), (QG, qo), (KG, ko), (VG, vo)):
        sent(sem, ref.at[pl.ds(0, F - 1)])

    def sent_but_own(stays, sem, ref, n):
        @pl.when(stays)
        def _():
            sent(sem, ref.at[pl.ds(0, n)])

        @pl.when(jnp.logical_not(stays))
        def _():
            sent(sem, ref)

    sent_but_own(core == y // 2, CG, cb, F - 1)
    sent_but_own(core == y // 2, CX, cxo, F - 1)
    sent_but_own(core == keeper, A, wv.at[0, 0, 0], 48)
    sent(OG, ogv.at[0])
    sent(ATT, attr)
    sent(B1Y, wv.at[0, :, :, pl.ds(0, 48), first])
    sent(B1X, wv.at[pl.ds(0, 3), :, :, pl.ds(0, 16), second])
    for i in range(3):
        sent(B2X + i, wv.at[0, :, :, :, first])
        sent(B2Y + i, wv.at[:, :, :, pl.ds(0, 16), second])
    for s, (_, _, devices) in enumerate(stages):
        sent(RED + s, red.at[s, pl.ds(0, len(devices))])


def local(queries, key_states, value_states, head_scale, out_weight, frame_pattern, out_grad):
    anywhere = pl.BlockSpec(memory_space=pl.ANY)
    scalars = pl.BlockSpec(memory_space=pltpu.SMEM)
    slots = pltpu.VMEM((F, T, HDH), BF16)
    parts = pltpu.VMEM((2, F, T, HDH), F32)
    square = pltpu.VMEM((F, 2 * T, T), F32)
    row = jax.ShapeDtypeStruct((T, F * HDH), BF16)
    attended, query_grad, key_grad, value_grad, scale_grad = pl.pallas_call(
        body,
        out_shape=(
            jax.ShapeDtypeStruct((T, D), BF16),
            row,
            row,
            row,
            jax.ShapeDtypeStruct((1, F), F32),
        ),
        in_specs=[scalars, scalars] + [anywhere] * 5,
        out_specs=[anywhere] * 4 + [pl.BlockSpec(memory_space=pltpu.VMEM)],
        scratch_shapes=[
            pltpu.VMEM((4, 2, 2, 64, D), BF16),
            pltpu.VMEM((2, T, D), BF16),
            slots, slots, slots, slots,
            pltpu.VMEM((2, F // 2, T, HDH), BF16),
            slots,
            pltpu.VMEM((2, T, F // 2 * HDH), BF16),
            slots, slots, slots,
            parts, parts,
            square, square,
            pltpu.VMEM((2, T, D), F32),
            pltpu.VMEM((T, D), F32),
            pltpu.VMEM((T, D), BF16),
            pltpu.VMEM((5, 4, 8, HDH), F32),
            pltpu.VMEM((6, 8, HDH), F32),
            pltpu.SemaphoreType.DMA((N_SEM,)),
            pltpu.SemaphoreType.DMA((N_SEM,)),
            pltpu.SemaphoreType.DMA((5,)),
        ],
        compiler_params=pltpu.CompilerParams(
            collective_id=0, has_side_effects=True, vmem_limit_bytes=56 << 20
        ),
    )(
        frame_pattern.T,
        head_scale,
        queries[0, 0],
        key_states[0, 0],
        value_states[0, 0],
        out_grad[0, 0],
        out_weight,
    )
    return (
        attended[None, None],
        query_grad[None, None],
        key_grad[None, None],
        value_grad[None, None],
        scale_grad.reshape(F),
    )


def solution(mesh):
    rows = P("dp", "frame", None, None)
    return jax.shard_map(
        local,
        mesh=mesh,
        in_specs=(rows, rows, rows, P(), P("dp", None), P(), rows),
        out_specs=(rows, rows, rows, rows, P()),
        check_vma=False,
    )
```

```python
import math

import jax
import jax.numpy as jnp
from jax import lax
from jax.experimental import pallas as pl
from jax.experimental.pallas import tpu as pltpu
from jax.sharding import PartitionSpec as P

MESH = pl.DeviceIdType.MESH
F = 16
T = 128
HDH = 128
D = 3072
HALF = D // 2
BF16 = jnp.bfloat16
F32 = jnp.float32

A, B1Y, B1X, OG, Q, K, V, CG, CX, ATT, QG, KG, VG = range(13)
B2X, B2Y, RED = 13, 16, 19
N_SEM = 22
NT = (((1,), (1,)), ((), ()))
TN = (((0,), (0,)), ((), ()))


def body(
    pat, scale, q, k, v, og, w, att, qg, kg, vg, sg,
    wv, ogv, qb, kb, vb, cb, cgo, cxo, cxr, qo, ko, vo, kp, vp, plain, probs, attp, attr, attv, red, redo,
    ss, rs, ls,
):
    d, f = lax.axis_index("dp"), lax.axis_index("frame")
    x, zl, core = d // 8, lax.rem(d // 2, 4), lax.rem(d, 2)
    zh, y = f // 4, lax.rem(f, 4)
    z = zh * 4 + zl

    def at_frame(i):
        return (d, lax.rem(f + i, F))

    def at_x(i, other=0):
        return (lax.rem(x + i + 4, 4) * 8 + zl * 2 + (1 - core if other else core), f)

    def at_y(i):
        return (d, zh * 4 + lax.rem(y + i + 4, 4))

    def at_zh(i):
        return (d, lax.rem(zh + i + 4, 4) * 4 + y)

    def at_z(i, c=core):
        there = lax.rem(z + i + 16, 16)
        return (x * 8 + lax.rem(there, 4) * 2 + c, (there // 4) * 4 + y)

    sibling = (d + 1 - 2 * core, f)

    def on_core(c, t):
        return (d - core + c, t)

    def turn(i):
        m = lax.rem(i, 4)
        dz = 1 + 2 * m - 3 * (m // 2)
        return lax.rem(zh + dz, 4) * 4 + lax.rem(y + 1 + i // 4, 4)

    def send(src, dst, sem, device, recv=None):
        pltpu.make_async_remote_copy(
            src, dst, ss.at[sem], rs.at[sem if recv is None else recv], device_id=device, device_id_type=MESH
        ).start()

    def arrive(sem, ref):
        pltpu.make_async_copy(ref, ref, rs.at[sem]).wait()

    def sent(sem, ref):
        pltpu.make_async_copy(ref, ref, ss.at[sem]).wait()

    barrier = pltpu.get_barrier_semaphore()
    peers = [at_x(i, c) for i in (1, 2, 3) for c in (0, 1)] + [at_z(i, c) for i in (1, -1, 2, -2) for c in (0, 1)] + [sibling]

    @pl.loop(1, F)
    def _(i):
        t = lax.rem(f + i, F)
        for c in (0, 1):
            pl.semaphore_signal(barrier, inc=1, device_id=on_core(c, t), device_id_type=MESH)

    for peer in peers:
        pl.semaphore_signal(barrier, inc=1, device_id=peer, device_id_type=MESH)
    pl.semaphore_wait(barrier, 2 * (F - 1) + len(peers))

    rows = pl.ds(pl.multiple_of(y * 16, 16), 16)
    first, second = pl.ds(0, HALF), pl.ds(HALF, HALF)
    mine = pl.ds(pl.multiple_of(f * HDH, HDH), HDH)

    keeper = zl // 2
    quarter = wv.at[x, lax.rem(zl, 2), core, rows]
    for i in (1, -1, 2):
        send(w.at[rows], quarter, A, at_z(i, keeper))

    @pl.when(core == keeper)
    def _():
        pltpu.make_async_copy(w.at[rows], quarter, rs.at[A]).start()

    @pl.when(core != keeper)
    def _():
        send(w.at[rows], quarter, A, sibling)

    pltpu.make_async_copy(og, ogv.at[core], ls.at[0]).start()
    send(og, ogv.at[core], OG, sibling)

    def scatter(src, dst, sem):
        @pl.loop(0, F - 1)
        def _(i):
            there = turn(i)
            send(src.at[:, pl.ds(pl.multiple_of(there * HDH, HDH), HDH)], dst.at[f], sem, (d, there))

        pltpu.make_async_copy(src.at[:, mine], dst.at[f], rs.at[sem]).start()

    scatter(q, qb, Q)
    scatter(k, kb, K)

    arrive(A, wv.at[x, :, :, rows])
    for i in (1, 2, 3):
        send(wv.at[x, :, :, rows, first], wv.at[x, :, :, rows, first], B1Y, at_y(i))
        send(wv.at[x, :, :, rows, second], wv.at[x, :, :, rows, second], B1X, at_x(i))

    arrive(B1Y, wv.at[x, :, :, pl.ds(0, 48), first])
    for i in (1, 2, 3):
        send(wv.at[x, :, :, :, first], wv.at[x, :, :, :, first], B2X + i - 1, at_x(i))
    arrive(B1X, wv.at[pl.ds(0, 3), :, :, rows, second])
    for i in (1, 2, 3):
        send(wv.at[:, :, :, rows, second], wv.at[:, :, :, rows, second], B2Y + i - 1, at_y(i))
    scatter(v, vb, V)

    inv_root = 1.0 / math.sqrt(HDH)
    factor = scale[f] * inv_root

    here = pl.ds(pl.multiple_of((zh * 2 + lax.rem(y, 2)) * HDH, HDH), HDH)

    def both(ref, t):
        return jnp.concatenate([ref[t], ref[pat[1, t]]], axis=0)

    arrive(Q, qb)
    arrive(K, kb)

    @pl.loop(0, F)
    def _(t):
        scores = lax.dot_general(both(kb, t), qb[t], NT, preferred_element_type=F32)
        plain[t] = scores
        scaled = scores * factor
        e = jnp.exp(scaled - jnp.max(scaled, axis=0, keepdims=True))
        probs[t] = e / jnp.sum(e, axis=0, keepdims=True)

    for i in (1, 2, 3):
        arrive(B2X + i - 1, wv.at[0, :, :, :, first])
        arrive(B2Y + i - 1, wv.at[:, :, :, pl.ds(0, 16), second])
    pltpu.make_async_copy(og, ogv.at[core], ls.at[0]).wait()
    arrive(OG, ogv.at[0])

    @pl.loop(0, 4)
    def _(i):
        dz = 1 + 2 * i - 3 * (i // 2)
        zh_head = lax.rem(zh + dz, 4)
        two = wv[zh_head].reshape(2 * HDH, D)
        made = lax.dot_general(ogv[...].reshape(2 * T, D), two, NT, preferred_element_type=F32).astype(BF16)
        for e in (0, 1):
            head = zh_head * 4 + 2 * core + e
            for c in (0, 1):
                piece = cgo.at[c, 2 * zh_head + e]
                piece[...] = made[c * T : (c + 1) * T, e * HDH : (e + 1) * HDH]
                stays = jnp.logical_and(core == c, head == f)

                @pl.when(stays)
                def _():
                    pltpu.make_async_copy(piece, cb.at[f], rs.at[CG]).start()

                @pl.when(jnp.logical_not(stays))
                def _():
                    send(piece, cb.at[f], CG, on_core(c, head))

    arrive(V, vb)

    def forward(t):
        return lax.dot_general(probs[t].astype(BF16), both(vb, t), TN, preferred_element_type=F32).astype(BF16)

    @pl.loop(0, F - 1)
    def _(i):
        t = turn(i)
        cxo[t] = forward(t)
        send(cxo.at[t], cxr.at[core, :, here], CX, on_core(y // 2, t))

    cxo[f] = forward(f)

    @pl.when(core == y // 2)
    def _():
        pltpu.make_async_copy(cxo.at[f], cxr.at[core, :, here], rs.at[CX]).start()

    @pl.when(core != y // 2)
    def _():
        send(cxo.at[f], cxr.at[core, :, here], CX, sibling)

    arrive(CG, cb)

    def backward(t):
        p = probs[t]
        gain = cb[t]
        prob_grad = lax.dot_general(both(vb, t), gain, NT, preferred_element_type=F32)
        score_grad = p * (prob_grad - jnp.sum(prob_grad * p, axis=0, keepdims=True))
        term = jnp.sum((score_grad * plain[t]).reshape(32, 8, HDH), axis=0)
        low = score_grad.astype(BF16)
        query = lax.dot_general(low, both(kb, t), TN, preferred_element_type=F32) * factor
        key = jnp.dot(low, qb[t], preferred_element_type=F32) * factor
        value = jnp.dot(p.astype(BF16), gain, preferred_element_type=F32)
        kp[0, t], kp[1, t] = key[:T], key[T:]
        vp[0, t], vp[1, t] = value[:T], value[T:]
        qo[t] = query.astype(BF16)
        return term

    redo[0] = jnp.zeros((8, HDH), F32)

    @pl.loop(0, F - 1)
    def _(i):
        t = turn(i)
        redo[0] += backward(t)
        send(qo.at[t], qg.at[:, mine], QG, (d, t))

    total = jnp.sum(redo[0] + backward(f), keepdims=True) * inv_root
    pltpu.make_async_copy(qo.at[f], qg.at[:, mine], ls.at[1]).start()

    lanes = lax.broadcasted_iota(jnp.int32, (8, HDH), 1)
    stages = (
        (F, f, [at_frame(i) for i in range(1, F)]),
        (8, x * 2 + core, [at_x(i, c) for i in range(4) for c in (0, 1) if (i, c) != (0, 0)]),
        (4, zl, [at_z(i) for i in (1, -1, 2)]),
    )

    def give(s, value):
        _, here, devices = stages[s]
        redo[s + 1] = value
        red[s, here] = value
        for device in devices:
            send(redo.at[s + 1], red.at[s, here], RED + s, device)

    def take(s):
        n, _, devices = stages[s]
        arrive(RED + s, red.at[s, pl.ds(0, len(devices))])
        return sum(red[s, j] for j in range(1, n)) + red[s, 0]

    give(0, jnp.where(lanes == f, total, 0.0))

    arrive(CX, cxr)
    width = 512

    @pl.loop(0, D // width)
    def _(n):
        cols = pl.ds(pl.multiple_of(n * width, width), width)
        block = wv[:, :, :, :, cols].reshape(F // 2 * HDH, width)
        made = jnp.dot(cxr[...].reshape(2 * T, F // 2 * HDH), block, preferred_element_type=F32)
        attp[:, :, cols] = made.reshape(2, T, width)

    send(attp.at[1 - core], attr, ATT, sibling)

    def gather(part, out, dst, sem, local):
        def one(g):
            acc = part[0, g]
            for t in range(F):
                acc += jnp.where(pat[1, t] == g, 1.0, 0.0) * part[1, t]
            out[g] = acc.astype(BF16)

        @pl.loop(0, F - 1)
        def _(i):
            g = turn(i)
            one(g)
            send(out.at[g], dst.at[:, mine], sem, (d, g))

        one(f)
        pltpu.make_async_copy(out.at[f], dst.at[:, mine], ls.at[local]).start()

    gather(kp, ko, kg, KG, 2)
    give(1, take(0))
    gather(vp, vo, vg, VG, 3)
    give(2, take(1))

    arrive(ATT, attr)
    attv[...] = (attp[core] + attr[...]).astype(BF16)
    pltpu.make_async_copy(attv, att, ls.at[0]).start()
    sg[...] = take(2)[:1, :F]

    for sem, ref in ((QG, qg), (KG, kg), (VG, vg)):
        arrive(sem, ref.at[:, pl.ds(0, (F - 1) * HDH)])
    for j, (src, dst) in enumerate(((qo, qg), (ko, kg), (vo, vg))):
        pltpu.make_async_copy(src.at[f], dst.at[:, mine], ls.at[j + 1]).wait()
    pltpu.make_async_copy(attv, att, ls.at[0]).wait()
    for sem, ref in ((Q, qb), (K, kb), (V, vb), (QG, qo), (KG, ko), (VG, vo)):
        sent(sem, ref.at[pl.ds(0, F - 1)])

    def sent_but_own(stays, sem, ref, n):
        @pl.when(stays)
        def _():
            sent(sem, ref.at[pl.ds(0, n)])

        @pl.when(jnp.logical_not(stays))
        def _():
            sent(sem, ref)

    sent_but_own(core == y // 2, CG, cb, F - 1)
    sent_but_own(core == y // 2, CX, cxo, F - 1)
    sent_but_own(core == keeper, A, wv.at[0, 0, 0], 48)
    sent(OG, ogv.at[0])
    sent(ATT, attr)
    sent(B1Y, wv.at[0, :, :, pl.ds(0, 48), first])
    sent(B1X, wv.at[pl.ds(0, 3), :, :, pl.ds(0, 16), second])
    for i in range(3):
        sent(B2X + i, wv.at[0, :, :, :, first])
        sent(B2Y + i, wv.at[:, :, :, pl.ds(0, 16), second])
    for s, (_, _, devices) in enumerate(stages):
        sent(RED + s, red.at[s, pl.ds(0, len(devices))])


def settle(*refs):
    scale, scale_out, sems = refs[4], refs[9], refs[14]
    arrays = list(zip(refs[:4], refs[10:14], refs[5:9]))
    copies = [pltpu.make_async_copy(src, held, sems.at[0, j]) for j, (src, held, _) in enumerate(arrays)]
    copies_out = [pltpu.make_async_copy(held, dst, sems.at[1, j]) for j, (_, held, dst) in enumerate(arrays)]
    for copy in copies:
        copy.start()
    scale_out[...] = scale[...]
    for copy, copy_out in zip(copies, copies_out):
        copy.wait()
        copy_out.start()
    for copy_out in copies_out:
        copy_out.wait()


def local(queries, key_states, value_states, head_scale, out_weight, frame_pattern, out_grad):
    anywhere = pl.BlockSpec(memory_space=pl.ANY)
    scalars = pl.BlockSpec(memory_space=pltpu.SMEM)
    slots = pltpu.VMEM((F, T, HDH), BF16)
    parts = pltpu.VMEM((2, F, T, HDH), F32)
    square = pltpu.VMEM((F, 2 * T, T), F32)
    row = jax.ShapeDtypeStruct((T, F * HDH), BF16)
    out_shape = (jax.ShapeDtypeStruct((T, D), BF16), row, row, row, jax.ShapeDtypeStruct((1, F), F32))
    vector = pl.BlockSpec(memory_space=pltpu.VMEM)
    made = pl.pallas_call(
        body,
        out_shape=out_shape,
        in_specs=[scalars, scalars] + [anywhere] * 5,
        out_specs=[anywhere] * 4 + [vector],
        scratch_shapes=[
            pltpu.VMEM((4, 2, 2, 64, D), BF16),
            pltpu.VMEM((2, T, D), BF16),
            slots, slots, slots, slots,
            pltpu.VMEM((2, F // 2, T, HDH), BF16),
            slots,
            pltpu.VMEM((2, T, F // 2 * HDH), BF16),
            slots, slots, slots,
            parts, parts,
            square, square,
            pltpu.VMEM((2, T, D), F32),
            pltpu.VMEM((T, D), F32),
            pltpu.VMEM((T, D), BF16),
            pltpu.VMEM((3, F, 8, HDH), F32),
            pltpu.VMEM((4, 8, HDH), F32),
            pltpu.SemaphoreType.DMA((N_SEM,)),
            pltpu.SemaphoreType.DMA((N_SEM,)),
            pltpu.SemaphoreType.DMA((4,)),
        ],
        compiler_params=pltpu.CompilerParams(
            collective_id=0, has_side_effects=True, vmem_limit_bytes=56 << 20
        ),
    )(
        frame_pattern.T,
        head_scale,
        queries[0, 0],
        key_states[0, 0],
        value_states[0, 0],
        out_grad[0, 0],
        out_weight,
    )
    attended, query_grad, key_grad, value_grad, scale_grad = pl.pallas_call(
        settle,
        out_shape=out_shape,
        in_specs=[anywhere] * 4 + [vector],
        out_specs=[anywhere] * 4 + [vector],
        scratch_shapes=[pltpu.VMEM((T, D), BF16)] + [pltpu.VMEM((T, F * HDH), BF16)] * 3 + [pltpu.SemaphoreType.DMA((2, 4))],
        compiler_params=pltpu.CompilerParams(vmem_limit_bytes=56 << 20),
    )(*made)
    return (
        attended[None, None],
        query_grad[None, None],
        key_grad[None, None],
        value_grad[None, None],
        scale_grad.reshape(F),
    )


def solution(mesh):
    rows = P("dp", "frame", None, None)
    return jax.shard_map(
        local,
        mesh=mesh,
        in_specs=(rows, rows, rows, P(), P("dp", None), P(), rows),
        out_specs=(rows, rows, rows, rows, P()),
        check_vma=False,
    )
```

```python
import math

import jax
import jax.numpy as jnp
from jax import lax
from jax.experimental import pallas as pl
from jax.experimental.pallas import tpu as pltpu
from jax.sharding import PartitionSpec as P

MESH = pl.DeviceIdType.MESH
F = 16
T = 128
HDH = 128
D = 3072
HALF = D // 2
BF16 = jnp.bfloat16
F32 = jnp.float32

A, B1Y, B1X, OG, Q, K, V, CG, CX, ATT, QG, KG, VG = range(13)
B2X, B2Y, RED = 13, 16, 19
N_SEM = 22
NT = (((1,), (1,)), ((), ()))
TN = (((0,), (0,)), ((), ()))


def body(
    pat, scale, q, k, v, og, w, att, qg, kg, vg, sg,
    wv, ogv, qb, kb, vb, cb, cgo, cxo, cxr, qo, ko, vo, kp, vp, plain, probs, attp, attr, attv, red, redo,
    ss, rs, ls,
):
    d, f = lax.axis_index("dp"), lax.axis_index("frame")
    x, zl, core = d // 8, lax.rem(d // 2, 4), lax.rem(d, 2)
    zh, y = f // 4, lax.rem(f, 4)
    z = zh * 4 + zl

    def at_frame(i):
        return (d, lax.rem(f + i, F))

    def at_x(i, other=0):
        return (lax.rem(x + i + 4, 4) * 8 + zl * 2 + (1 - core if other else core), f)

    def at_y(i):
        return (d, zh * 4 + lax.rem(y + i + 4, 4))

    def at_zh(i):
        return (d, lax.rem(zh + i + 4, 4) * 4 + y)

    def at_z(i, c=core):
        there = lax.rem(z + i + 16, 16)
        return (x * 8 + lax.rem(there, 4) * 2 + c, (there // 4) * 4 + y)

    sibling = (d + 1 - 2 * core, f)

    def on_core(c, t):
        return (d - core + c, t)

    def turn(i):
        m = lax.rem(i, 4)
        dz = 1 + 2 * m - 3 * (m // 2)
        return lax.rem(zh + dz, 4) * 4 + lax.rem(y + 1 + i // 4, 4)

    def send(src, dst, sem, device, recv=None):
        pltpu.make_async_remote_copy(
            src, dst, ss.at[sem], rs.at[sem if recv is None else recv], device_id=device, device_id_type=MESH
        ).start()

    def arrive(sem, ref):
        pltpu.make_async_copy(ref, ref, rs.at[sem]).wait()

    def sent(sem, ref):
        pltpu.make_async_copy(ref, ref, ss.at[sem]).wait()

    barrier = pltpu.get_barrier_semaphore()
    peers = [at_x(i, c) for i in (1, 2, 3) for c in (0, 1)] + [at_z(i, c) for i in (1, -1, 2, -2) for c in (0, 1)] + [sibling]

    @pl.loop(1, F)
    def _(i):
        t = lax.rem(f + i, F)
        for c in (0, 1):
            pl.semaphore_signal(barrier, inc=1, device_id=on_core(c, t), device_id_type=MESH)

    for peer in peers:
        pl.semaphore_signal(barrier, inc=1, device_id=peer, device_id_type=MESH)
    pl.semaphore_wait(barrier, 2 * (F - 1) + len(peers))

    rows = pl.ds(pl.multiple_of(y * 16, 16), 16)
    first, second = pl.ds(0, HALF), pl.ds(HALF, HALF)
    mine = pl.ds(pl.multiple_of(f * HDH, HDH), HDH)

    keeper = zl // 2
    quarter = wv.at[x, lax.rem(zl, 2), core, rows]
    for i in (1, -1, 2):
        send(w.at[rows], quarter, A, at_z(i, keeper))

    @pl.when(core == keeper)
    def _():
        pltpu.make_async_copy(w.at[rows], quarter, rs.at[A]).start()

    @pl.when(core != keeper)
    def _():
        send(w.at[rows], quarter, A, sibling)

    pltpu.make_async_copy(og, ogv.at[core], ls.at[0]).start()
    send(og, ogv.at[core], OG, sibling)

    def scatter(src, dst, sem):
        @pl.loop(0, F - 1)
        def _(i):
            there = turn(i)
            send(src.at[:, pl.ds(pl.multiple_of(there * HDH, HDH), HDH)], dst.at[f], sem, (d, there))

        pltpu.make_async_copy(src.at[:, mine], dst.at[f], rs.at[sem]).start()

    scatter(q, qb, Q)
    scatter(k, kb, K)

    arrive(A, wv.at[x, :, :, rows])
    for i in (1, 2, 3):
        send(wv.at[x, :, :, rows, first], wv.at[x, :, :, rows, first], B1Y, at_y(i))
        send(wv.at[x, :, :, rows, second], wv.at[x, :, :, rows, second], B1X, at_x(i))

    arrive(B1Y, wv.at[x, :, :, pl.ds(0, 48), first])
    for i in (1, 2, 3):
        send(wv.at[x, :, :, :, first], wv.at[x, :, :, :, first], B2X + i - 1, at_x(i))
    arrive(B1X, wv.at[pl.ds(0, 3), :, :, rows, second])
    for i in (1, 2, 3):
        send(wv.at[:, :, :, rows, second], wv.at[:, :, :, rows, second], B2Y + i - 1, at_y(i))
    scatter(v, vb, V)

    inv_root = 1.0 / math.sqrt(HDH)
    factor = scale[f] * inv_root

    here = pl.ds(pl.multiple_of((zh * 2 + lax.rem(y, 2)) * HDH, HDH), HDH)

    def both(ref, t):
        return jnp.concatenate([ref[t], ref[pat[1, t]]], axis=0)

    arrive(Q, qb)
    arrive(K, kb)

    @pl.loop(0, F)
    def _(t):
        scores = lax.dot_general(both(kb, t), qb[t], NT, preferred_element_type=F32)
        plain[t] = scores
        scaled = scores * factor
        e = jnp.exp(scaled - jnp.max(scaled, axis=0, keepdims=True))
        probs[t] = e / jnp.sum(e, axis=0, keepdims=True)

    for i in (1, 2, 3):
        arrive(B2X + i - 1, wv.at[0, :, :, :, first])
        arrive(B2Y + i - 1, wv.at[:, :, :, pl.ds(0, 16), second])
    pltpu.make_async_copy(og, ogv.at[core], ls.at[0]).wait()
    arrive(OG, ogv.at[0])

    @pl.loop(0, 4)
    def _(i):
        dz = 1 + 2 * i - 3 * (i // 2)
        zh_head = lax.rem(zh + dz, 4)
        two = wv[zh_head].reshape(2 * HDH, D)
        made = lax.dot_general(ogv[...].reshape(2 * T, D), two, NT, preferred_element_type=F32).astype(BF16)
        for e in (0, 1):
            head = zh_head * 4 + 2 * core + e
            for c in (0, 1):
                piece = cgo.at[c, 2 * zh_head + e]
                piece[...] = made[c * T : (c + 1) * T, e * HDH : (e + 1) * HDH]
                stays = jnp.logical_and(core == c, head == f)

                @pl.when(stays)
                def _():
                    pltpu.make_async_copy(piece, cb.at[f], rs.at[CG]).start()

                @pl.when(jnp.logical_not(stays))
                def _():
                    send(piece, cb.at[f], CG, on_core(c, head))

    arrive(V, vb)

    def forward(t):
        return lax.dot_general(probs[t].astype(BF16), both(vb, t), TN, preferred_element_type=F32).astype(BF16)

    @pl.loop(0, F - 1)
    def _(i):
        t = turn(i)
        cxo[t] = forward(t)
        send(cxo.at[t], cxr.at[core, :, here], CX, on_core(y // 2, t))

    cxo[f] = forward(f)

    @pl.when(core == y // 2)
    def _():
        pltpu.make_async_copy(cxo.at[f], cxr.at[core, :, here], rs.at[CX]).start()

    @pl.when(core != y // 2)
    def _():
        send(cxo.at[f], cxr.at[core, :, here], CX, sibling)

    arrive(CG, cb)

    def backward(t):
        p = probs[t]
        gain = cb[t]
        prob_grad = lax.dot_general(both(vb, t), gain, NT, preferred_element_type=F32)
        score_grad = p * (prob_grad - jnp.sum(prob_grad * p, axis=0, keepdims=True))
        term = jnp.sum((score_grad * plain[t]).reshape(32, 8, HDH), axis=0)
        low = score_grad.astype(BF16)
        query = lax.dot_general(low, both(kb, t), TN, preferred_element_type=F32) * factor
        key = jnp.dot(low, qb[t], preferred_element_type=F32) * factor
        value = jnp.dot(p.astype(BF16), gain, preferred_element_type=F32)
        kp[0, t], kp[1, t] = key[:T], key[T:]
        vp[0, t], vp[1, t] = value[:T], value[T:]
        qo[t] = query.astype(BF16)
        return term

    redo[0] = jnp.zeros((8, HDH), F32)

    @pl.loop(0, F - 1)
    def _(i):
        t = turn(i)
        redo[0] += backward(t)
        send(qo.at[t], qg.at[:, mine], QG, (d, t))

    total = jnp.sum(redo[0] + backward(f), keepdims=True) * inv_root
    pltpu.make_async_copy(qo.at[f], qg.at[:, mine], ls.at[1]).start()

    lanes = lax.broadcasted_iota(jnp.int32, (8, HDH), 1)
    stages = (
        (F, f, [at_frame(i) for i in range(1, F)]),
        (8, x * 2 + core, [at_x(i, c) for i in range(4) for c in (0, 1) if (i, c) != (0, 0)]),
        (4, zl, [at_z(i) for i in (1, -1, 2)]),
    )

    def give(s, value):
        _, here, devices = stages[s]
        redo[s + 1] = value
        red[s, here] = value
        for device in devices:
            send(redo.at[s + 1], red.at[s, here], RED + s, device)

    def take(s):
        n, _, devices = stages[s]
        arrive(RED + s, red.at[s, pl.ds(0, len(devices))])
        return sum(red[s, j] for j in range(1, n)) + red[s, 0]

    give(0, jnp.where(lanes == f, total, 0.0))

    arrive(CX, cxr)
    width = 512

    @pl.loop(0, D // width)
    def _(n):
        cols = pl.ds(pl.multiple_of(n * width, width), width)
        block = wv[:, :, :, :, cols].reshape(F // 2 * HDH, width)
        made = jnp.dot(cxr[...].reshape(2 * T, F // 2 * HDH), block, preferred_element_type=F32)
        attp[:, :, cols] = made.reshape(2, T, width)

    send(attp.at[1 - core], attr, ATT, sibling)

    def gather(part, out, dst, sem, local):
        def one(g):
            acc = part[0, g]
            for t in range(F):
                acc += jnp.where(pat[1, t] == g, 1.0, 0.0) * part[1, t]
            out[g] = acc.astype(BF16)

        @pl.loop(0, F - 1)
        def _(i):
            g = turn(i)
            one(g)
            send(out.at[g], dst.at[:, mine], sem, (d, g))

        one(f)
        pltpu.make_async_copy(out.at[f], dst.at[:, mine], ls.at[local]).start()

    gather(kp, ko, kg, KG, 2)
    give(1, take(0))
    gather(vp, vo, vg, VG, 3)
    give(2, take(1))

    arrive(ATT, attr)
    attv[...] = (attp[core] + attr[...]).astype(BF16)
    pltpu.make_async_copy(attv, att, ls.at[0]).start()
    sg[...] = take(2)[:1, :F]

    for sem, ref in ((QG, qg), (KG, kg), (VG, vg)):
        arrive(sem, ref.at[:, pl.ds(0, (F - 1) * HDH)])
    for j, (src, dst) in enumerate(((qo, qg), (ko, kg), (vo, vg))):
        pltpu.make_async_copy(src.at[f], dst.at[:, mine], ls.at[j + 1]).wait()
    pltpu.make_async_copy(attv, att, ls.at[0]).wait()
    for sem, ref in ((Q, qb), (K, kb), (V, vb), (QG, qo), (KG, ko), (VG, vo)):
        sent(sem, ref.at[pl.ds(0, F - 1)])

    def sent_but_own(stays, sem, ref, n):
        @pl.when(stays)
        def _():
            sent(sem, ref.at[pl.ds(0, n)])

        @pl.when(jnp.logical_not(stays))
        def _():
            sent(sem, ref)

    sent_but_own(core == y // 2, CG, cb, F - 1)
    sent_but_own(core == y // 2, CX, cxo, F - 1)
    sent_but_own(core == keeper, A, wv.at[0, 0, 0], 48)
    sent(OG, ogv.at[0])
    sent(ATT, attr)
    sent(B1Y, wv.at[0, :, :, pl.ds(0, 48), first])
    sent(B1X, wv.at[pl.ds(0, 3), :, :, pl.ds(0, 16), second])
    for i in range(3):
        sent(B2X + i, wv.at[0, :, :, :, first])
        sent(B2Y + i, wv.at[:, :, :, pl.ds(0, 16), second])
    for s, (_, _, devices) in enumerate(stages):
        sent(RED + s, red.at[s, pl.ds(0, len(devices))])


def settle(*refs):
    scale, scale_out, sems = refs[4], refs[9], refs[14]
    halves = [pl.ds(n * T // 2, T // 2) for n in (0, 1)]
    arrays = [(i.at[n], v.at[n], o.at[n]) for i, v, o in zip(refs[:4], refs[10:14], refs[5:9]) for n in halves]
    copies = [pltpu.make_async_copy(src, held, sems.at[0, j]) for j, (src, held, _) in enumerate(arrays)]
    copies_out = [pltpu.make_async_copy(held, dst, sems.at[1, j]) for j, (_, held, dst) in enumerate(arrays)]
    for copy in copies:
        copy.start()
    scale_out[...] = scale[...]
    for copy, copy_out in zip(copies, copies_out):
        copy.wait()
        copy_out.start()
    for copy_out in copies_out:
        copy_out.wait()


def local(queries, key_states, value_states, head_scale, out_weight, frame_pattern, out_grad):
    anywhere = pl.BlockSpec(memory_space=pl.ANY)
    scalars = pl.BlockSpec(memory_space=pltpu.SMEM)
    slots = pltpu.VMEM((F, T, HDH), BF16)
    parts = pltpu.VMEM((2, F, T, HDH), F32)
    square = pltpu.VMEM((F, 2 * T, T), F32)
    row = jax.ShapeDtypeStruct((T, F * HDH), BF16)
    out_shape = (jax.ShapeDtypeStruct((T, D), BF16), row, row, row, jax.ShapeDtypeStruct((1, F), F32))
    vector = pl.BlockSpec(memory_space=pltpu.VMEM)
    made = pl.pallas_call(
        body,
        out_shape=out_shape,
        in_specs=[scalars, scalars] + [anywhere] * 5,
        out_specs=[anywhere] * 4 + [vector],
        scratch_shapes=[
            pltpu.VMEM((4, 2, 2, 64, D), BF16),
            pltpu.VMEM((2, T, D), BF16),
            slots, slots, slots, slots,
            pltpu.VMEM((2, F // 2, T, HDH), BF16),
            slots,
            pltpu.VMEM((2, T, F // 2 * HDH), BF16),
            slots, slots, slots,
            parts, parts,
            square, square,
            pltpu.VMEM((2, T, D), F32),
            pltpu.VMEM((T, D), F32),
            pltpu.VMEM((T, D), BF16),
            pltpu.VMEM((3, F, 8, HDH), F32),
            pltpu.VMEM((4, 8, HDH), F32),
            pltpu.SemaphoreType.DMA((N_SEM,)),
            pltpu.SemaphoreType.DMA((N_SEM,)),
            pltpu.SemaphoreType.DMA((4,)),
        ],
        compiler_params=pltpu.CompilerParams(
            collective_id=0, has_side_effects=True, vmem_limit_bytes=56 << 20
        ),
    )(
        frame_pattern.T,
        head_scale,
        queries[0, 0],
        key_states[0, 0],
        value_states[0, 0],
        out_grad[0, 0],
        out_weight,
    )
    attended, query_grad, key_grad, value_grad, scale_grad = pl.pallas_call(
        settle,
        out_shape=out_shape,
        in_specs=[anywhere] * 4 + [vector],
        out_specs=[anywhere] * 4 + [vector],
        scratch_shapes=[pltpu.VMEM((T, D), BF16)] + [pltpu.VMEM((T, F * HDH), BF16)] * 3 + [pltpu.SemaphoreType.DMA((2, 8))],
        compiler_params=pltpu.CompilerParams(vmem_limit_bytes=56 << 20),
    )(*made)
    return (
        attended[None, None],
        query_grad[None, None],
        key_grad[None, None],
        value_grad[None, None],
        scale_grad.reshape(F),
    )


def solution(mesh):
    rows = P("dp", "frame", None, None)
    return jax.shard_map(
        local,
        mesh=mesh,
        in_specs=(rows, rows, rows, P(), P("dp", None), P(), rows),
        out_specs=(rows, rows, rows, rows, P()),
        check_vma=False,
    )
```
